512 devices in a mesh: pipe: 8 (over z), ctx: 32 (over x, y_hi, core), tp: 2 (over y_lo).
Axes of the slice: x: 4, y: 8 (y_hi: 4, y_lo: 2; y = y_hi * 2 + y_lo), z: 8, core: 2. Of those that a mesh axis runs over, the one named last changes fastest.
Arguments:
- queries: bfloat16 [8, 2048, 128, 128], P('pipe', 'ctx', 'tp'), may hold values from -10 to 10
- span_keys: bfloat16 [8, 2048, 8, 128], P('pipe', 'ctx', 'tp'), may hold values from -6 to 6
- span_values: bfloat16 [8, 2048, 8, 128], P('pipe', 'ctx', 'tp'), may hold values from -12 to 12
- cache_keys: bfloat16 [8, 1024, 8, 128], P('pipe', 'ctx', 'tp'), may hold values from -6 to 6
- cache_values: bfloat16 [8, 1024, 8, 128], P('pipe', 'ctx', 'tp'), may hold values from -6 to 6
- scale_exps: int32 [8, 64, 8, 2], P('pipe', 'ctx', 'tp'), may hold values from -3 to 1
- block_order: int32 [8, 64], P('pipe'), may hold values from 0 to 63, each once within a row
Outputs:
- handed: bfloat16 [8, 2048, 128, 128], P('pipe', 'ctx', 'tp')
The draws below stay inside these ranges and needn't reach their ends.
All inputs are finite; a program needn't handle non-finite values.
Results may differ from the reference program's by a relative error of at most 0.006.
Values may be sent and summed in bfloat16 or wider, within the bound.
No kernel may reach another device: no remote copies, remote signals or barrier semaphores. Data moves between devices by JAX's collectives and lax.ppermute only.
A program may use at most 128 MiB of HBM per device.

```python
import jax
import jax.numpy as jnp
from jax import lax

HEADS = 128
KVH = 8
HD = 128
CBLK = 16
GROUP = 16
SECTS = 8
HALF = 32
SPAN = 2048
CTXT = 1024
NBLK = 64
OWNERS = 64


def joint_draw(key):
    keys = jnp.clip(1.5 * jax.random.normal(jax.random.fold_in(key, 11), (SECTS, SPAN, KVH, HD), jnp.float32), -6.0, 6.0)
    query = jnp.clip(jax.random.normal(jax.random.fold_in(key, 12), (SECTS, SPAN, HEADS, HD), jnp.float32), -6.0, 6.0)
    return (query, keys)


def draw_queries(key, part):
    return joint_draw(key)[0].astype(jnp.bfloat16)


def draw_span_keys(key, part):
    return joint_draw(key)[1].astype(jnp.bfloat16)


def plant(values, key, least, largest):
    dims = values.shape
    place = [jax.random.randint(jax.random.fold_in(key, axis), (), 0, dims[axis]) for axis in range(len(dims))]
    values = values.at[tuple(place)].set(least)
    longest = dims.index(max(dims))
    place[longest] = (place[longest] + 1) % dims[longest]
    return values.at[tuple(place)].set(largest)


def level_of(stream_key, shape, shards, smallest, top_value):
    level, own = 1.0, jax.random.fold_in(stream_key, 6)
    for dim, parts in shards:
        draws = jnp.exp(jax.random.uniform(jax.random.fold_in(own, dim), (parts,), jnp.float32, smallest / len(shards), top_value / len(shards)))
        level = level * jnp.repeat(draws, shape[dim] // parts).reshape([-1 if axis == dim else 1 for axis in range(len(shape))])
    return level


def centred(key, shape, scale, limit, cuts=(), kind=jnp.bfloat16):
    array = jax.random.normal(key, shape, jnp.float32) * scale
    if len(cuts) > 0:
        array = level_of(key, shape, cuts, -0.22, 0.18) * array
    return jnp.clip(array, min=-limit, max=limit).astype(kind)


def setup_inputs(seed: int = 0) -> dict:
    key_list = jax.random.split(jax.random.key(seed), 8)
    queries = draw_queries(jax.random.fold_in(key_list[7], 71), 0)
    span_keys = draw_span_keys(jax.random.fold_in(key_list[7], 71), 0)
    span_values = centred(key_list[2], (SECTS, SPAN, KVH, HD), 2.0, 12.0, ((0, 8), (1, 32), (2, 2)))
    cache_keys = centred(key_list[3], (SECTS, CTXT, KVH, HD), 1.0, 6.0, ((0, 8), (1, 32), (2, 2)))
    cache_values = centred(key_list[4], (SECTS, CTXT, KVH, HD), 1.0, 6.0, ((0, 8), (1, 32), (2, 2)))
    scale_exps = plant(jax.random.randint(key_list[5], (SECTS, NBLK, KVH, 2), -3, 2), jax.random.fold_in(key_list[5], 1), -3, 1).astype(jnp.int32)
    block_order = jax.vmap(lambda own: jax.random.permutation(own, OWNERS))(jax.random.split(key_list[6], SECTS)).reshape((SECTS, OWNERS)).astype(jnp.int32)
    return dict(queries=queries, span_keys=span_keys, span_values=span_values, cache_keys=cache_keys, cache_values=cache_values, scale_exps=scale_exps, block_order=block_order)


def hadamard(order):
    rows = jnp.arange(order, dtype=jnp.int32)[:, None]
    cols = jnp.arange(order, dtype=jnp.int32)[None, :]
    common = jnp.zeros((order, order), jnp.int32)
    for bit in range(order.bit_length() - 1):
        common = common + (jnp.right_shift(rows, bit) & 1) * (jnp.right_shift(cols, bit) & 1)
    signs = 1.0 - 2.0 * (common % 2).astype(jnp.float32)
    return signs * (1.0 / (order ** 0.5))


def section(query, ckeys, cvalues, kcache, vcache, exps, order):
    factor = jnp.repeat(jnp.exp2(exps.astype(jnp.float32)), CBLK, axis=0)
    keys_ctx = (kcache.astype(jnp.float32) * factor[:, :, 0:1]).astype(jnp.bfloat16)
    vals_ctx = (vcache.astype(jnp.float32) * factor[:, :, 1:2]).astype(jnp.bfloat16)
    keys = jnp.concatenate([keys_ctx, ckeys], axis=0)
    vals = jnp.concatenate([vals_ctx, cvalues], axis=0)
    count = query.shape[0]
    index = jnp.arange(count, dtype=jnp.int32)
    position = order[index // HALF] * HALF + index % HALF
    visible = jnp.concatenate([jnp.ones((count, CTXT), bool), position[None, :] <= position[:, None]], axis=1)
    grouped = query.reshape(count, KVH, GROUP, HD)
    inv = 1.0 / (HD ** 0.5)

    def one_head(head):
        qhead = grouped[:, head].astype(jnp.float32)
        khead = keys[:, head].astype(jnp.float32)
        vhead = vals[:, head].astype(jnp.float32)
        score = jnp.einsum('tqd,kd->qtk', qhead, khead) * inv
        score = jnp.where(visible[None], score, -jnp.inf)
        top = jnp.max(score, axis=-1, keepdims=True)
        expo = jnp.exp(score - top)
        total = jnp.sum(expo, axis=-1)
        weight = expo.astype(jnp.bfloat16).astype(jnp.float32)
        return jnp.einsum('qtk,kd->qtd', weight, vhead) / total[..., None]

    mixed = lax.map(one_head, jnp.arange(KVH, dtype=jnp.int32))
    rotated = jnp.dot(mixed.reshape(-1, HD), hadamard(HD), precision=lax.Precision.HIGHEST)
    rotated = rotated.reshape(KVH, GROUP, count, HD).transpose(2, 0, 1, 3)
    return rotated.reshape(count, HEADS, HD).astype(jnp.bfloat16)


def reference(queries, span_keys, span_values, cache_keys, cache_values, scale_exps, block_order):
    outs = []
    for sect in range(SECTS):
        outs.append(section(queries[sect], span_keys[sect], span_values[sect], cache_keys[sect], cache_values[sect], scale_exps[sect], block_order[sect]))
    result = jnp.stack(outs, axis=0)
    return jnp.roll(result, 1, axis=0)
```

```python
import functools
import math

import jax
import jax.numpy as jnp
from jax import lax
from jax.experimental import pallas as pl
from jax.experimental.pallas import tpu as pltpu
from jax.sharding import Mesh, PartitionSpec as P


CBLK = 16
HALF = 32
HD = 128
GROUP = 16
FAR = -(2.0**100)
FLAT = ("pipe", "x", "y", "core")


def moved(value, sizes, dz=0, dx=0, dc=0):
    nz, nx, ny, nc = sizes
    pairs = []
    for z in range(nz):
        for x in range(nx):
            for y in range(ny):
                for c in range(nc):
                    source = ((z * nx + x) * ny + y) * nc + c
                    target = ((((z + dz) % nz) * nx + (x + dx) % nx) * ny + y) * nc + (c ^ dc)
                    pairs.append((source, target))
    return lax.ppermute(value, FLAT, pairs)


def iota(shape, axis):
    return lax.broadcasted_iota(jnp.int32, shape, axis)


def pick(rows, width, first, per_head, heads, scale=None):
    out = iota((rows, width), 0)
    src = iota((rows, width), 1)
    head = first + out // per_head
    token = out % per_head
    hit = src == token * heads + head
    if scale is None:
        return jnp.where(hit, 1.0, 0.0).astype(jnp.bfloat16)
    return jnp.where(hit, scale(token // CBLK, head), 0.0).astype(jnp.bfloat16)


def pack_body(core_ref, exps_ref, sk_ref, sv_ref, ck_ref, cv_ref, own_ref, other_ref, *, heads):
    core = core_ref[0]
    tok = sk_ref.shape[0] // heads
    cache = ck_ref.shape[0] // heads
    for which, ref in ((0, own_ref), (1, other_ref)):
        first = 2 * (core if which == 0 else 1 - core)
        span_pick = pick(2 * tok, heads * tok, first, tok, heads)
        for kv, (span, cached) in enumerate(((sk_ref, ck_ref), (sv_ref, cv_ref))):

            def scale(block, head):
                value = jnp.ones(block.shape, jnp.float32)
                for b in range(cache // CBLK):
                    for h in range(heads):
                        power = (jnp.int32(1) << (exps_ref[b, kv, h] + 3)).astype(jnp.float32) * 0.125
                        value = jnp.where((block == b) & (head == h), power, value)
                return value

            cache_pick = pick(2 * cache, heads * cache, first, cache, heads, scale)
            moved_span = jnp.dot(span_pick, span[...], preferred_element_type=jnp.float32).astype(jnp.bfloat16)
            moved_cache = jnp.dot(cache_pick, cached[...], preferred_element_type=jnp.float32).astype(jnp.bfloat16)
            for h in range(2):
                ref[h, kv, :cache] = moved_cache[h * cache : (h + 1) * cache]
                ref[h, kv, cache:] = moved_span[h * tok : (h + 1) * tok]


def pack(core, exps, span_keys, span_values, cache_keys, cache_values):
    tok, heads, width = span_keys.shape
    cache = cache_keys.shape[0]
    flat = lambda a: a.reshape(-1, width)
    shape = jax.ShapeDtypeStruct((2, 2, cache + tok, width), jnp.bfloat16)
    smem = pl.BlockSpec(memory_space=pltpu.SMEM)
    vmem = pl.BlockSpec(memory_space=pltpu.VMEM)
    return pl.pallas_call(
        functools.partial(pack_body, heads=heads),
        out_shape=(shape, shape),
        in_specs=[smem, smem, vmem, vmem, vmem, vmem],
        out_specs=(vmem, vmem),
        compiler_params=pltpu.CompilerParams(vmem_limit_bytes=8 << 20),
        name="pack_kv",
    )(core, exps, flat(span_keys), flat(span_values), flat(cache_keys), flat(cache_values))


def fill(place_ref, order_ref, chunk_refs, spots, ka, va, head_slot, tok, cache):
    x, y, core = place_ref[0], place_ref[1], place_ref[2]
    nx, ny = place_ref[3], place_ref[4]
    halves = tok // HALF
    lane = iota((HALF, HD), 1)
    within = iota((HALF, HD), 0)
    slot = lane // HALF
    base = jnp.zeros((HALF, HD), jnp.int32)
    for s in range(2 * halves):
        owner = (x * ny + y) * 2 + (core if s < halves else 1 - core)
        base = jnp.where(slot == s, order_ref[0, owner * halves + s % halves], base)
    pos_query = base * HALF + lane % HALF
    rows = cache + tok
    at = 0
    for ref, spot in zip(chunk_refs, spots):
        count = ref.shape[0]
        shift, first_y = spot
        src_x = (x + shift) % nx
        for k in range(count):
            for cc in range(2):
                owner = (src_x * ny + first_y + k) * 2 + (core if cc == 0 else 1 - core)
                ka[at : at + rows, :HD] = ref[k, cc, head_slot, 0]
                va[at : at + rows, :HD] = ref[k, cc, head_slot, 1]
                ka[at : at + cache, HD:] = jnp.zeros((cache, HD), jnp.bfloat16)
                for b in range(halves):
                    pos_key = order_ref[0, owner * halves + b] * HALF + within
                    start = at + cache + b * HALF
                    ka[start : start + HALF, HD:] = jnp.where(pos_key <= pos_query, 0.0, FAR).astype(jnp.bfloat16)
                at += rows
    va[:, HD:] = jnp.ones((va.shape[0], HD), jnp.bfloat16)


def stage_body(*refs, nq, nchunk, spots, first, last, tok, cache, tile_tok, sub):
    place_ref, order_ref = refs[0], refs[1]
    refs = refs[2:]
    q_refs, refs = refs[:nq], refs[nq:]
    chunk_refs, refs = refs[:nchunk], refs[nchunk:]
    if not first:
        (acc_in, max_in), refs = refs[:2], refs[2:]
    if last:
        (own_ref, other_ref), refs = refs[:2], refs[2:]
    else:
        (acc_out, max_out), refs = refs[:2], refs[2:]
    ka, va = refs
    head = pl.program_id(0)
    tile = pl.program_id(1)

    @pl.when(tile == 0)
    def _():
        fill(place_ref, order_ref, chunk_refs, spots, ka, va, head, tok, cache)

    rows = tile_tok * GROUP
    factor = math.log2(math.e) / math.sqrt(HD)
    if last:
        i, j = iota((HD, HD), 0), iota((HD, HD), 1)
        bits = i & j
        bits = bits ^ (bits >> 4)
        bits = bits ^ (bits >> 2)
        bits = (bits ^ (bits >> 1)) & 1
        signs = (1.0 - 2.0 * bits.astype(jnp.float32)).astype(jnp.bfloat16)
        signs = jnp.concatenate([signs, signs], axis=0)
    for s in range(rows // sub):
        tok0 = s * sub // GROUP
        tok1 = (s + 1) * sub // GROUP
        part = q_refs[0][tok0:tok1].reshape(sub, HD)
        if nq == 2:
            other = q_refs[1][tok0:tok1].reshape(sub, HD)
            part = jnp.where(tile < tok // tile_tok, part, other)
        token = tile * tile_tok + tok0 + iota((sub, HD), 0) // GROUP
        hot = jnp.where(iota((sub, HD), 1) == token, 1.0, 0.0).astype(jnp.bfloat16)
        left = jnp.concatenate([part, hot], axis=1)
        score = lax.dot_general(left, ka[...], (((1,), (1,)), ((), ())), preferred_element_type=jnp.float32)
        top = jnp.max(score, axis=1, keepdims=True)
        span = slice(s * sub, (s + 1) * sub)
        if not first:
            top_old = max_in[0, span, :1]
            top = jnp.maximum(top, top_old)
        weight = jnp.exp2((score - top) * factor).astype(jnp.bfloat16)
        acc = jnp.dot(weight, va[...], preferred_element_type=jnp.float32)
        if not first:
            acc = acc + acc_in[0, span] * jnp.exp2((top_old - top) * factor)
        if last:
            mixed = acc[:, :HD] / (acc[:, HD:] * math.sqrt(HD))
            high = mixed.astype(jnp.bfloat16)
            low = (mixed - high.astype(jnp.float32)).astype(jnp.bfloat16)
            turned = jnp.dot(jnp.concatenate([high, low], axis=1), signs, preferred_element_type=jnp.float32)
            turned = turned.astype(jnp.bfloat16).reshape(sub // GROUP, GROUP, HD)

            @pl.when(tile < tok // tile_tok)
            def _():
                own_ref[tok0:tok1] = turned

            @pl.when(tile >= tok // tile_tok)
            def _():
                other_ref[tok0:tok1] = turned
        else:
            acc_out[0, span] = acc
            max_out[0, span] = jnp.broadcast_to(top, (sub, HD))


def stage(place, order, queries, chunks, spots, state, tok, cache, last=False, tile_tok=64, sub=256):
    nq = len(queries)
    per = queries[0].shape[0] // tile_tok
    tiles = nq * per
    rows = tile_tok * GROUP
    total = 2 * tok * GROUP
    keys = sum(c.shape[0] for c in chunks) * 2 * (cache + tok)
    smem = pl.BlockSpec(memory_space=pltpu.SMEM)
    first = state is None
    in_specs = [smem]
    for n in range(nq):
        in_specs.append(pl.BlockSpec((tile_tok, GROUP, HD), lambda h, t, p, n=n: (jnp.clip(t - n * per, 0, per - 1), h, 0)))
    for c in chunks:
        in_specs.append(pl.BlockSpec(c.shape, lambda h, t, p, nd=c.ndim: (0,) * nd, pipeline_mode=pl.Buffered(1)))
    acc_spec = pl.BlockSpec((1, rows, 2 * HD), lambda h, t, p: (h, t, 0))
    max_spec = pl.BlockSpec((1, rows, HD), lambda h, t, p: (h, t, 0))
    operands = [order, *queries, *chunks]
    if not first:
        in_specs += [acc_spec, max_spec]
        operands += list(state)
    if last:
        out_specs = (
            pl.BlockSpec((tile_tok, GROUP, HD), lambda h, t, p: (jnp.minimum(t, per - 1), 2 * p[2] + h, 0)),
            pl.BlockSpec((tile_tok, GROUP, HD), lambda h, t, p: (jnp.maximum(t - per, 0), h, 0)),
        )
        out_shape = (
            jax.ShapeDtypeStruct((tok, 4 * GROUP, HD), jnp.bfloat16),
            jax.ShapeDtypeStruct((tok, 2 * GROUP, HD), jnp.bfloat16),
        )
    else:
        out_specs = (acc_spec, max_spec)
        out_shape = (
            jax.ShapeDtypeStruct((2, total, 2 * HD), jnp.float32),
            jax.ShapeDtypeStruct((2, total, HD), jnp.float32),
        )
    body = functools.partial(
        stage_body, nq=nq, nchunk=len(chunks), spots=spots, first=first, last=last, tok=tok, cache=cache,
        tile_tok=tile_tok, sub=sub,
    )
    return pl.pallas_call(
        body,
        grid_spec=pltpu.PrefetchScalarGridSpec(
            num_scalar_prefetch=1,
            grid=(2, tiles),
            in_specs=in_specs,
            out_specs=out_specs,
            scratch_shapes=[pltpu.VMEM((keys, 2 * HD), jnp.bfloat16), pltpu.VMEM((keys, 2 * HD), jnp.bfloat16)],
        ),
        out_shape=out_shape,
        compiler_params=pltpu.CompilerParams(vmem_limit_bytes=32 << 20),
        name="stage_last" if last else "stage",
    )(place, *operands)


def put_body(place_ref, part_ref, whole_ref, out_ref, sem):
    heads = part_ref.shape[1]
    copy = pltpu.make_async_copy(part_ref, out_ref.at[:, pl.ds((1 - place_ref[2]) * heads, heads)], sem)
    copy.start()
    copy.wait()


def put(place, part, whole):
    raw = pl.BlockSpec(memory_space=pl.ANY)
    return pl.pallas_call(
        put_body,
        out_shape=jax.ShapeDtypeStruct(whole.shape, whole.dtype),
        in_specs=[pl.BlockSpec(memory_space=pltpu.SMEM), raw, raw],
        out_specs=raw,
        scratch_shapes=[pltpu.SemaphoreType.DMA],
        input_output_aliases={2: 0},
        compiler_params=pltpu.CompilerParams(vmem_limit_bytes=1 << 20),
        name="put",
    )(place, part, whole)


def on_device(queries, span_keys, span_values, cache_keys, cache_values, scale_exps, block_order, sizes):
    return relay(queries, span_keys, span_values, cache_keys, cache_values, scale_exps, block_order, sizes)


def relay(queries, span_keys, span_values, cache_keys, cache_values, scale_exps, block_order, sizes):
    _, nx, ny, nc = sizes
    tok, heads, width = queries.shape[1:]
    cache = cache_keys.shape[1]
    core = lax.axis_index("core").astype(jnp.int32)
    place = jnp.stack([lax.axis_index("x").astype(jnp.int32), lax.axis_index("y").astype(jnp.int32), core, jnp.int32(nx), jnp.int32(ny)])
    exps = scale_exps[0].transpose(0, 2, 1)
    own, other = pack(core.reshape(1), exps, span_keys[0], span_values[0], cache_keys[0], cache_values[0])
    own = moved(own, sizes, dz=1)
    other = moved(other, sizes, dz=1, dc=1)
    order = moved(block_order, sizes, dz=1)
    half_heads = heads // 2
    q_own = lax.dynamic_slice_in_dim(queries[0], core * half_heads, half_heads, 1)
    q_other = lax.dynamic_slice_in_dim(queries[0], (1 - core) * half_heads, half_heads, 1)
    q_own = moved(q_own, sizes, dz=1)
    q_other = moved(q_other, sizes, dz=1, dc=1)
    rows = 2 * 2 * (cache + tok)
    mine = jnp.concatenate([own.reshape(rows, width), other.reshape(rows, width)], axis=0)
    line = lax.all_gather(mine, "y", axis=0, tiled=True)
    parts = lambda a: a.reshape(-1, nc, 2, 2, cache + tok, width)
    half = line.shape[0] // 2
    before = moved(line, sizes, dx=1)
    after = moved(line, sizes, dx=-1)
    state = stage(place, order, [q_own, q_other], [parts(line)], [(0, 0)], None, tok, cache)
    far_a = moved(before[:half], sizes, dx=1)
    far_b = moved(after[half:], sizes, dx=-1)
    state = stage(place, order, [q_own, q_other], [parts(before), parts(after)], [(nx - 1, 0), (1, 0)], state, tok, cache)
    final = [parts(far_a), parts(far_b)]
    spots = [(2, 0), (2, ny // 2)]
    result, theirs = stage(place, order, [q_own, q_other], final, spots, state, tok, cache, last=True)
    theirs = moved(theirs, sizes, dc=1)
    return put(place, theirs, result)[None]


def solution(mesh):
    nz, nctx, ntp = mesh.devices.shape
    nx = ny = 4
    nc = nctx // (nx * ny)
    fine = Mesh(mesh.devices.reshape(nz, nx, ny, nc, ntp), ("pipe", "x", "y", "core", "tp"))
    split = P("pipe", ("x", "y", "core"), "tp", None)
    return jax.shard_map(
        functools.partial(on_device, sizes=(nz, nx, ny, nc)),
        mesh=fine,
        in_specs=(split,) * 6 + (P("pipe", None),),
        out_specs=split,
        check_vma=False,
    )
```

```python
import functools
import math

import jax
import jax.numpy as jnp
from jax import lax
from jax.experimental import pallas as pl
from jax.experimental.pallas import tpu as pltpu
from jax.sharding import Mesh, PartitionSpec as P


CBLK = 16
HALF = 32
HD = 128
GROUP = 16
FAR = -(2.0**100)
FLAT = ("pipe", "x", "y", "core")


def moved(value, sizes, dz=0, dx=0, dc=0):
    nz, nx, ny, nc = sizes
    pairs = []
    for z in range(nz):
        for x in range(nx):
            for y in range(ny):
                for c in range(nc):
                    source = ((z * nx + x) * ny + y) * nc + c
                    target = ((((z + dz) % nz) * nx + (x + dx) % nx) * ny + y) * nc + (c ^ dc)
                    pairs.append((source, target))
    return lax.ppermute(value, FLAT, pairs)


def iota(shape, axis):
    return lax.broadcasted_iota(jnp.int32, shape, axis)


def pick(rows, width, first, per_head, heads, scale=None):
    out = iota((rows, width), 0)
    src = iota((rows, width), 1)
    head = first + out // per_head
    token = out % per_head
    hit = src == token * heads + head
    if scale is None:
        return jnp.where(hit, 1.0, 0.0).astype(jnp.bfloat16)
    return jnp.where(hit, scale(token // CBLK, head), 0.0).astype(jnp.bfloat16)


def pack_body(core_ref, exps_ref, order_ref, sk_ref, sv_ref, ck_ref, cv_ref, own_ref, other_ref, *, heads):
    core = core_ref[0]
    tok = sk_ref.shape[0] // heads
    cache = ck_ref.shape[0] // heads
    for which, ref in ((0, own_ref), (1, other_ref)):
        first = 2 * (core if which == 0 else 1 - core)
        span_pick = pick(2 * tok, heads * tok, first, tok, heads)
        for kv, (span, cached) in enumerate(((sk_ref, ck_ref), (sv_ref, cv_ref))):

            def scale(block, head):
                value = jnp.ones(block.shape, jnp.float32)
                for b in range(cache // CBLK):
                    for h in range(heads):
                        power = (jnp.int32(1) << (exps_ref[b, kv, h] + 3)).astype(jnp.float32) * 0.125
                        value = jnp.where((block == b) & (head == h), power, value)
                return value

            cache_pick = pick(2 * cache, heads * cache, first, cache, heads, scale)
            moved_span = jnp.dot(span_pick, span[...], preferred_element_type=jnp.float32).astype(jnp.bfloat16)
            moved_cache = jnp.dot(cache_pick, cached[...], preferred_element_type=jnp.float32).astype(jnp.bfloat16)
            for h in range(2):
                at = (2 * h + kv) * (cache + tok)
                ref[at : at + cache] = moved_cache[h * cache : (h + 1) * cache]
                ref[at + cache : at + cache + tok] = moved_span[h * tok : (h + 1) * tok]
    order = order_ref[...].astype(jnp.float32)
    order = jnp.concatenate([order, jnp.zeros((1, HD - order.shape[1]), jnp.float32)], axis=1)
    own_ref[4 * (cache + tok) :] = jnp.broadcast_to(order, (16, HD)).astype(jnp.bfloat16)


def pack(core, exps, order, span_keys, span_values, cache_keys, cache_values):
    tok, heads, width = span_keys.shape
    cache = cache_keys.shape[0]
    flat = lambda a: a.reshape(-1, width)
    rows = 4 * (cache + tok)
    smem = pl.BlockSpec(memory_space=pltpu.SMEM)
    vmem = pl.BlockSpec(memory_space=pltpu.VMEM)
    return pl.pallas_call(
        functools.partial(pack_body, heads=heads),
        out_shape=(jax.ShapeDtypeStruct((rows + 16, width), jnp.bfloat16), jax.ShapeDtypeStruct((rows, width), jnp.bfloat16)),
        in_specs=[smem, smem, vmem, vmem, vmem, vmem, vmem],
        out_specs=(vmem, vmem),
        name="pack_kv",
    )(core, exps, order, flat(span_keys), flat(span_values), flat(cache_keys), flat(cache_values))


def fill(place_ref, order_ref, chunk_refs, spots, ka, va, head_slot, tok, cache):
    x, y, core = place_ref[0], place_ref[1], place_ref[2]
    nx, ny = place_ref[3], place_ref[4]
    halves = tok // HALF
    lane = iota((HALF, HD), 1)
    within = iota((HALF, HD), 0)
    slot = lane // HALF
    base = jnp.zeros((HALF, HD), jnp.int32)
    for s in range(2 * halves):
        owner = (x * ny + y) * 2 + (core if s < halves else 1 - core)
        base = jnp.where(slot == s, order_ref[0, owner * halves + s % halves], base)
    pos_query = base * HALF + lane % HALF
    rows = cache + tok
    at = 0
    for ref, spot in zip(chunk_refs, spots):
        count = ref.shape[0]
        shift, first_y = spot
        src_x = (x + shift) % nx
        for k in range(count):
            for cc in range(2):
                owner = (src_x * ny + first_y + k) * 2 + (core if cc == 0 else 1 - core)
                ka[at : at + rows, :HD] = ref[k, cc, head_slot, 0]
                va[at : at + rows, :HD] = ref[k, cc, head_slot, 1]
                ka[at : at + cache, HD:] = jnp.zeros((cache, HD), jnp.bfloat16)
                for b in range(halves):
                    pos_key = order_ref[0, owner * halves + b] * HALF + within
                    start = at + cache + b * HALF
                    ka[start : start + HALF, HD:] = jnp.where(pos_key <= pos_query, 0.0, FAR).astype(jnp.bfloat16)
                at += rows
    va[:, HD:] = jnp.ones((va.shape[0], HD), jnp.bfloat16)


def stage_body(*refs, nchunk, spots, first, last, tok, cache, sub, ahead, lag):
    place_ref, order_ref = refs[0], refs[1]
    refs = refs[2:]
    q_refs, refs = refs[:2], refs[2:]
    chunk_refs, refs = refs[:nchunk], refs[nchunk:]
    if not first:
        (acc_in, max_in), refs = refs[:2], refs[2:]
    if last:
        (own_ref, other_ref), refs = refs[:2], refs[2:]
    else:
        (acc_out, max_out), refs = refs[:2], refs[2:]
    ka, va = refs
    fill(place_ref, order_ref, chunk_refs, spots, ka, va, pl.program_id(0), tok, cache)
    factor = math.log2(math.e) / math.sqrt(HD)
    if last:
        i, j = iota((HD, HD), 0), iota((HD, HD), 1)
        bits = i & j
        bits = bits ^ (bits >> 4)
        bits = bits ^ (bits >> 2)
        bits = (bits ^ (bits >> 1)) & 1
        signs = (1.0 - 2.0 * bits.astype(jnp.float32)).astype(jnp.bfloat16)
        signs = jnp.concatenate([signs, signs], axis=0)
    toks = sub // GROUP
    pieces = 2 * tok // toks

    def scores(s):
        tok0 = s * toks
        ref = q_refs[tok0 // tok]
        part = ref[tok0 % tok : tok0 % tok + toks].reshape(sub, HD)
        token = tok0 + iota((sub, HD), 0) // GROUP
        hot = jnp.where(iota((sub, HD), 1) == token, 1.0, 0.0).astype(jnp.bfloat16)
        left = jnp.concatenate([part, hot], axis=1)
        return lax.dot_general(left, ka[...], (((1,), (1,)), ((), ())), preferred_element_type=jnp.float32)

    def finish(s, acc):
        mixed = acc[:, :HD] * (1.0 / (acc[:, HD:] * math.sqrt(HD)))
        high = mixed.astype(jnp.bfloat16)
        low = (mixed - high.astype(jnp.float32)).astype(jnp.bfloat16)
        turned = jnp.dot(jnp.concatenate([high, low], axis=1), signs, preferred_element_type=jnp.float32)
        turned = turned.astype(jnp.bfloat16).reshape(toks, GROUP, HD)
        ref = (own_ref, other_ref)[s * toks // tok]
        ref[s * toks % tok : s * toks % tok + toks] = turned

    ready = [scores(s) for s in range(ahead)]
    waiting = []
    for s in range(pieces):
        if s + ahead < pieces:
            ready.append(scores(s + ahead))
        score = ready[s]
        ready[s] = None
        span = slice(s * sub, (s + 1) * sub)
        top = jnp.max(score, axis=1, keepdims=True)
        if not first:
            top_old = max_in[0, span, :1]
            top = jnp.maximum(top, top_old)
        weight = jnp.exp2((score - top) * factor).astype(jnp.bfloat16)
        acc = jnp.dot(weight, va[...], preferred_element_type=jnp.float32)
        if not first:
            acc = acc + acc_in[0, span] * jnp.exp2((top_old - top) * factor)
        if last:
            waiting.append((s, acc))
            if len(waiting) > lag:
                finish(*waiting.pop(0))
        else:
            acc_out[0, span] = acc
            max_out[0, span] = jnp.broadcast_to(top, (sub, HD))
    for item in waiting:
        finish(*item)


def stage(place, order, queries, chunks, spots, state, tok, cache, last=False, sub=512, ahead=1, lag=1):
    total = 2 * tok * GROUP
    keys = sum(c.shape[0] for c in chunks) * 2 * (cache + tok)
    first = state is None
    in_specs = [pl.BlockSpec(memory_space=pltpu.SMEM)]
    for _ in queries:
        in_specs.append(pl.BlockSpec((tok, GROUP, HD), lambda h, p: (0, 2 * p[2] + h, 0)))
    for c in chunks:
        in_specs.append(pl.BlockSpec(c.shape, lambda h, p, nd=c.ndim: (0,) * nd, pipeline_mode=pl.Buffered(1)))
    acc_spec = pl.BlockSpec((1, total, 2 * HD), lambda h, p: (h, 0, 0))
    max_spec = pl.BlockSpec((1, total, HD), lambda h, p: (h, 0, 0))
    operands = [order, *queries, *chunks]
    if not first:
        in_specs += [acc_spec, max_spec]
        operands += list(state)
    if last:
        out_specs = (
            pl.BlockSpec((tok, GROUP, HD), lambda h, p: (0, 2 * p[2] + h, 0)),
            pl.BlockSpec((tok, GROUP, HD), lambda h, p: (0, h, 0)),
        )
        out_shape = (
            jax.ShapeDtypeStruct((tok, 4 * GROUP, HD), jnp.bfloat16),
            jax.ShapeDtypeStruct((tok, 2 * GROUP, HD), jnp.bfloat16),
        )
    else:
        out_specs = (acc_spec, max_spec)
        out_shape = (
            jax.ShapeDtypeStruct((2, total, 2 * HD), jnp.float32),
            jax.ShapeDtypeStruct((2, total, HD), jnp.float32),
        )
    body = functools.partial(
        stage_body, nchunk=len(chunks), spots=spots, first=first, last=last, tok=tok, cache=cache, sub=sub, ahead=ahead, lag=lag
    )
    return pl.pallas_call(
        body,
        grid_spec=pltpu.PrefetchScalarGridSpec(
            num_scalar_prefetch=1,
            grid=(2,),
            in_specs=in_specs,
            out_specs=out_specs,
            scratch_shapes=[pltpu.VMEM((keys, 2 * HD), jnp.bfloat16), pltpu.VMEM((keys, 2 * HD), jnp.bfloat16)],
        ),
        out_shape=out_shape,
        compiler_params=pltpu.CompilerParams(vmem_limit_bytes=36 << 20),
        name="stage_last" if last else "stage",
    )(place, *operands)


def put_body(place_ref, part_ref, whole_ref, out_ref, sem):
    heads = part_ref.shape[1]
    copy = pltpu.make_async_copy(part_ref, out_ref.at[:, pl.ds((1 - place_ref[2]) * heads, heads)], sem)
    copy.start()
    copy.wait()


def put(place, part, whole):
    raw = pl.BlockSpec(memory_space=pl.ANY)
    return pl.pallas_call(
        put_body,
        out_shape=jax.ShapeDtypeStruct(whole.shape, whole.dtype),
        in_specs=[pl.BlockSpec(memory_space=pltpu.SMEM), raw, raw],
        out_specs=raw,
        scratch_shapes=[pltpu.SemaphoreType.DMA],
        input_output_aliases={2: 0},
        compiler_params=pltpu.CompilerParams(vmem_limit_bytes=1 << 20),
        name="put",
    )(place, part, whole)


def on_device(queries, span_keys, span_values, cache_keys, cache_values, scale_exps, block_order, sizes):
    return relay(queries, span_keys, span_values, cache_keys, cache_values, scale_exps, block_order, sizes)


def relay(queries, span_keys, span_values, cache_keys, cache_values, scale_exps, block_order, sizes):
    _, nx, ny, nc = sizes
    tok, _, width = queries.shape[1:]
    cache = cache_keys.shape[1]
    core = lax.axis_index("core").astype(jnp.int32)
    place = jnp.stack([lax.axis_index("x").astype(jnp.int32), lax.axis_index("y").astype(jnp.int32), core, jnp.int32(nx), jnp.int32(ny)])
    exps = scale_exps[0].transpose(0, 2, 1)
    own, other = pack(core.reshape(1), exps, block_order, span_keys[0], span_values[0], cache_keys[0], cache_values[0])
    own = moved(own, sizes, dz=1)
    other = moved(other, sizes, dz=1, dc=1)
    rows = 4 * (cache + tok)
    order = own[rows : rows + 1, : block_order.shape[1]].astype(jnp.int32)
    q_own = moved(queries[0], sizes, dz=1)
    q_other = moved(q_own, sizes, dc=1)
    mine = jnp.concatenate([own[:rows], other], axis=0)
    line = lax.all_gather(mine, "y", axis=0, tiled=True)
    parts = lambda a: a.reshape(-1, nc, 2, 2, cache + tok, width)
    half = line.shape[0] // 2
    before = moved(line, sizes, dx=1)
    after = moved(line, sizes, dx=-1)
    state = stage(place, order, [q_own, q_other], [parts(line)], [(0, 0)], None, tok, cache)
    far_a = moved(before[:half], sizes, dx=1)
    far_b = moved(after[half:], sizes, dx=-1)
    state = stage(place, order, [q_own, q_other], [parts(before), parts(after)], [(nx - 1, 0), (1, 0)], state, tok, cache)
    final = [parts(far_a), parts(far_b)]
    spots = [(2, 0), (2, ny // 2)]
    result, theirs = stage(place, order, [q_own, q_other], final, spots, state, tok, cache, last=True, ahead=2)
    theirs = moved(theirs, sizes, dc=1)
    return put(place, theirs, result)[None]


def solution(mesh):
    nz, nctx, ntp = mesh.devices.shape
    nx = ny = 4
    nc = nctx // (nx * ny)
    fine = Mesh(mesh.devices.reshape(nz, nx, ny, nc, ntp), ("pipe", "x", "y", "core", "tp"))
    split = P("pipe", ("x", "y", "core"), "tp", None)
    return jax.shard_map(
        functools.partial(on_device, sizes=(nz, nx, ny, nc)),
        mesh=fine,
        in_specs=(split,) * 6 + (P("pipe", None),),
        out_specs=split,
        check_vma=False,
    )
```

```python
import functools
import math

import jax
import jax.numpy as jnp
from jax import lax
from jax.experimental import pallas as pl
from jax.experimental.pallas import tpu as pltpu
from jax.sharding import Mesh, PartitionSpec as P


CBLK = 16
HALF = 32
HD = 128
GROUP = 16
FAR = -(2.0**100)
FLAT = ("pipe", "x", "y", "core")


def moved(value, sizes, dz=0, dx=0, dc=0):
    nz, nx, ny, nc = sizes
    pairs = []
    for z in range(nz):
        for x in range(nx):
            for y in range(ny):
                for c in range(nc):
                    source = ((z * nx + x) * ny + y) * nc + c
                    target = ((((z + dz) % nz) * nx + (x + dx) % nx) * ny + y) * nc + (c ^ dc)
                    pairs.append((source, target))
    return lax.ppermute(value, FLAT, pairs)


def iota(shape, axis):
    return lax.broadcasted_iota(jnp.int32, shape, axis)


def pick(rows, width, first, per_head, heads, scale=None):
    out = iota((rows, width), 0)
    src = iota((rows, width), 1)
    head = first + out // per_head
    token = out % per_head
    hit = src == token * heads + head
    if scale is None:
        return jnp.where(hit, 1.0, 0.0).astype(jnp.bfloat16)
    return jnp.where(hit, scale(token // CBLK, head), 0.0).astype(jnp.bfloat16)


def pack_body(core_ref, exps_ref, order_ref, sk_ref, sv_ref, ck_ref, cv_ref, own_ref, other_ref, *, heads):
    core = core_ref[0]
    tok = sk_ref.shape[0] // heads
    cache = ck_ref.shape[0] // heads
    for which, ref in ((0, own_ref), (1, other_ref)):
        first = 2 * (core if which == 0 else 1 - core)
        span_pick = pick(2 * tok, heads * tok, first, tok, heads)
        for kv, (span, cached) in enumerate(((sk_ref, ck_ref), (sv_ref, cv_ref))):

            def scale(block, head):
                value = jnp.ones(block.shape, jnp.float32)
                for b in range(cache // CBLK):
                    for h in range(heads):
                        power = (jnp.int32(1) << (exps_ref[b, kv, h] + 3)).astype(jnp.float32) * 0.125
                        value = jnp.where((block == b) & (head == h), power, value)
                return value

            cache_pick = pick(2 * cache, heads * cache, first, cache, heads, scale)
            moved_span = jnp.dot(span_pick, span[...], preferred_element_type=jnp.float32).astype(jnp.bfloat16)
            moved_cache = jnp.dot(cache_pick, cached[...], preferred_element_type=jnp.float32).astype(jnp.bfloat16)
            for h in range(2):
                at = (2 * h + kv) * (cache + tok)
                ref[at : at + cache] = moved_cache[h * cache : (h + 1) * cache]
                ref[at + cache : at + cache + tok] = moved_span[h * tok : (h + 1) * tok]
    order = order_ref[...].astype(jnp.float32)
    order = jnp.concatenate([order, jnp.zeros((1, HD - order.shape[1]), jnp.float32)], axis=1)
    own_ref[4 * (cache + tok) :] = jnp.broadcast_to(order, (16, HD)).astype(jnp.bfloat16)


def pack(core, exps, order, span_keys, span_values, cache_keys, cache_values):
    tok, heads, width = span_keys.shape
    cache = cache_keys.shape[0]
    flat = lambda a: a.reshape(-1, width)
    rows = 4 * (cache + tok)
    smem = pl.BlockSpec(memory_space=pltpu.SMEM)
    vmem = pl.BlockSpec(memory_space=pltpu.VMEM)
    return pl.pallas_call(
        functools.partial(pack_body, heads=heads),
        out_shape=(jax.ShapeDtypeStruct((rows + 16, width), jnp.bfloat16), jax.ShapeDtypeStruct((rows, width), jnp.bfloat16)),
        in_specs=[smem, smem, vmem, vmem, vmem, vmem, vmem],
        out_specs=(vmem, vmem),
        name="pack_kv",
    )(core, exps, order, flat(span_keys), flat(span_values), flat(cache_keys), flat(cache_values))


def fill(place_ref, order_ref, chunk_refs, spots, ka, va, head_slot, tok, cache):
    x, y, core = place_ref[0], place_ref[1], place_ref[2]
    nx, ny = place_ref[3], place_ref[4]
    halves = tok // HALF
    lane = iota((HALF, HD), 1)
    within = iota((HALF, HD), 0)
    slot = lane // HALF
    base = jnp.zeros((HALF, HD), jnp.int32)
    for s in range(2 * halves):
        owner = (x * ny + y) * 2 + (core if s < halves else 1 - core)
        base = jnp.where(slot == s, order_ref[0, owner * halves + s % halves], base)
    pos_query = base * HALF + lane % HALF
    rows = cache + tok
    at = 0
    for ref, spot in zip(chunk_refs, spots):
        count = ref.shape[0]
        shift, first_y = spot
        src_x = (x + shift) % nx
        for k in range(count):
            for cc in range(2):
                owner = (src_x * ny + first_y + k) * 2 + (core if cc == 0 else 1 - core)
                ka[at : at + rows, :HD] = ref[k, cc, head_slot, 0]
                va[at : at + rows, :HD] = ref[k, cc, head_slot, 1]
                ka[at : at + cache, HD:] = jnp.zeros((cache, HD), jnp.bfloat16)
                for b in range(halves):
                    pos_key = order_ref[0, owner * halves + b] * HALF + within
                    start = at + cache + b * HALF
                    ka[start : start + HALF, HD:] = jnp.where(pos_key <= pos_query, 0.0, FAR).astype(jnp.bfloat16)
                at += rows
    va[:, HD:] = jnp.ones((va.shape[0], HD), jnp.bfloat16)


def stage_body(*refs, nchunk, spots, first, last, tok, cache, sub, ahead, lag):
    place_ref, order_ref = refs[0], refs[1]
    refs = refs[2:]
    q_refs, refs = refs[:2], refs[2:]
    chunk_refs, refs = refs[:nchunk], refs[nchunk:]
    if not first:
        (acc_in, max_in), refs = refs[:2], refs[2:]
    if last:
        (own_ref, other_ref), refs = refs[:2], refs[2:]
    else:
        (acc_out, max_out), refs = refs[:2], refs[2:]
    ka, va = refs
    fill(place_ref, order_ref, chunk_refs, spots, ka, va, pl.program_id(0), tok, cache)
    factor = math.log2(math.e) / math.sqrt(HD)
    if last:
        i, j = iota((HD, HD), 0), iota((HD, HD), 1)
        bits = i & j
        bits = bits ^ (bits >> 4)
        bits = bits ^ (bits >> 2)
        bits = (bits ^ (bits >> 1)) & 1
        signs = (1.0 - 2.0 * bits.astype(jnp.float32)).astype(jnp.bfloat16)
        signs = jnp.concatenate([signs, signs], axis=0)
    toks = sub // GROUP
    pieces = 2 * tok // toks

    def scores(s):
        tok0 = s * toks
        ref = q_refs[tok0 // tok]
        part = ref[tok0 % tok : tok0 % tok + toks].reshape(sub, HD)
        token = tok0 + iota((sub, HD), 0) // GROUP
        hot = jnp.where(iota((sub, HD), 1) == token, 1.0, 0.0).astype(jnp.bfloat16)
        left = jnp.concatenate([part, hot], axis=1)
        return lax.dot_general(left, ka[...], (((1,), (1,)), ((), ())), preferred_element_type=jnp.float32)

    def finish(s, acc):
        mixed = acc[:, :HD] * (1.0 / (acc[:, HD:] * math.sqrt(HD)))
        high = mixed.astype(jnp.bfloat16)
        low = (mixed - high.astype(jnp.float32)).astype(jnp.bfloat16)
        turned = jnp.dot(jnp.concatenate([high, low], axis=1), signs, preferred_element_type=jnp.float32)
        turned = turned.astype(jnp.bfloat16).reshape(toks, GROUP, HD)
        ref = (own_ref, other_ref)[s * toks // tok]
        ref[s * toks % tok : s * toks % tok + toks] = turned

    ready = [scores(s) for s in range(ahead)]
    waiting = []
    for s in range(pieces):
        if s + ahead < pieces:
            ready.append(scores(s + ahead))
        score = ready[s]
        ready[s] = None
        span = slice(s * sub, (s + 1) * sub)
        top = jnp.max(score, axis=1, keepdims=True)
        if not first:
            top_old = max_in[0, span, :1]
            top = jnp.maximum(top, top_old)
        weight = jnp.exp2((score - top) * factor).astype(jnp.bfloat16)
        acc = jnp.dot(weight, va[...], preferred_element_type=jnp.float32)
        if not first:
            acc = acc + acc_in[0, span] * jnp.exp2((top_old - top) * factor)
        if last:
            waiting.append((s, acc))
            if len(waiting) > lag:
                finish(*waiting.pop(0))
        else:
            acc_out[0, span] = acc
            max_out[0, span] = jnp.broadcast_to(top, (sub, HD))
    for item in waiting:
        finish(*item)


def stage(place, order, queries, chunks, spots, state, tok, cache, last=False, sub=512, ahead=1, lag=1):
    total = 2 * tok * GROUP
    keys = sum(c.shape[0] for c in chunks) * 2 * (cache + tok)
    first = state is None
    in_specs = [pl.BlockSpec(memory_space=pltpu.SMEM)]
    for _ in queries:
        in_specs.append(pl.BlockSpec((tok, GROUP, HD), lambda h, p: (0, 2 * p[2] + h, 0)))
    for c in chunks:
        in_specs.append(pl.BlockSpec(c.shape, lambda h, p, nd=c.ndim: (0,) * nd, pipeline_mode=pl.Buffered(1)))
    acc_spec = pl.BlockSpec((1, total, 2 * HD), lambda h, p: (h, 0, 0))
    max_spec = pl.BlockSpec((1, total, HD), lambda h, p: (h, 0, 0))
    operands = [order, *queries, *chunks]
    if not first:
        in_specs += [acc_spec, max_spec]
        operands += list(state)
    if last:
        out_specs = (
            pl.BlockSpec((tok, GROUP, HD), lambda h, p: (0, 2 * p[2] + h, 0)),
            pl.BlockSpec((tok, GROUP, HD), lambda h, p: (0, h, 0)),
        )
        out_shape = (
            jax.ShapeDtypeStruct((tok, 4 * GROUP, HD), jnp.bfloat16),
            jax.ShapeDtypeStruct((tok, 2 * GROUP, HD), jnp.bfloat16),
        )
    else:
        out_specs = (acc_spec, max_spec)
        out_shape = (
            jax.ShapeDtypeStruct((2, total, 2 * HD), jnp.float32),
            jax.ShapeDtypeStruct((2, total, HD), jnp.float32),
        )
    body = functools.partial(
        stage_body, nchunk=len(chunks), spots=spots, first=first, last=last, tok=tok, cache=cache, sub=sub, ahead=ahead, lag=lag
    )
    return pl.pallas_call(
        body,
        grid_spec=pltpu.PrefetchScalarGridSpec(
            num_scalar_prefetch=1,
            grid=(2,),
            in_specs=in_specs,
            out_specs=out_specs,
            scratch_shapes=[pltpu.VMEM((keys, 2 * HD), jnp.bfloat16), pltpu.VMEM((keys, 2 * HD), jnp.bfloat16)],
        ),
        out_shape=out_shape,
        compiler_params=pltpu.CompilerParams(vmem_limit_bytes=24 << 20),
        name="stage_last" if last else "stage",
    )(place, *operands)


def put_body(place_ref, part_ref, whole_ref, out_ref, sem):
    heads = part_ref.shape[1]
    copy = pltpu.make_async_copy(part_ref, out_ref.at[:, pl.ds((1 - place_ref[2]) * heads, heads)], sem)
    copy.start()
    copy.wait()


def put(place, part, whole):
    raw = pl.BlockSpec(memory_space=pl.ANY)
    return pl.pallas_call(
        put_body,
        out_shape=jax.ShapeDtypeStruct(whole.shape, whole.dtype),
        in_specs=[pl.BlockSpec(memory_space=pltpu.SMEM), raw, raw],
        out_specs=raw,
        scratch_shapes=[pltpu.SemaphoreType.DMA],
        input_output_aliases={2: 0},
        compiler_params=pltpu.CompilerParams(vmem_limit_bytes=1 << 20),
        name="put",
    )(place, part, whole)


def on_device(queries, span_keys, span_values, cache_keys, cache_values, scale_exps, block_order, sizes):
    return relay(queries, span_keys, span_values, cache_keys, cache_values, scale_exps, block_order, sizes)


def relay(queries, span_keys, span_values, cache_keys, cache_values, scale_exps, block_order, sizes):
    _, nx, ny, nc = sizes
    tok, _, width = queries.shape[1:]
    cache = cache_keys.shape[1]
    core = lax.axis_index("core").astype(jnp.int32)
    place = jnp.stack([lax.axis_index("x").astype(jnp.int32), lax.axis_index("y").astype(jnp.int32), core, jnp.int32(nx), jnp.int32(ny)])
    exps = scale_exps[0].transpose(0, 2, 1)
    own, other = pack(core.reshape(1), exps, block_order, span_keys[0], span_values[0], cache_keys[0], cache_values[0])
    own = moved(own, sizes, dz=1)
    other = moved(other, sizes, dz=1, dc=1)
    rows = 4 * (cache + tok)
    order = own[rows : rows + 1, : block_order.shape[1]].astype(jnp.int32)
    q_own = moved(queries[0], sizes, dz=1)
    q_other = moved(q_own, sizes, dc=1)
    mine = jnp.concatenate([own[:rows], other], axis=0)
    line = lax.all_gather(mine, "y", axis=0, tiled=True)
    parts = lambda a: a.reshape(-1, nc, 2, 2, cache + tok, width)
    half = line.shape[0] // 2
    low, high = line[:half], line[half:]
    near_a = moved(low, sizes, dx=1)
    near_b = moved(high, sizes, dx=-1)
    rest_a = moved(high, sizes, dx=1)
    rest_b = moved(low, sizes, dx=-1)
    far_a = moved(near_a, sizes, dx=1)
    far_b = moved(near_b, sizes, dx=-1)
    mid = ny // 2
    spots = [(0, 0), (nx - 1, 0), (1, mid)]
    state = stage(place, order, [q_own, q_other], [parts(line), parts(near_a), parts(near_b)], spots, None, tok, cache)
    chunks = [parts(rest_a), parts(rest_b), parts(far_a), parts(far_b)]
    spots = [(nx - 1, mid), (1, 0), (2, 0), (2, mid)]
    result, theirs = stage(place, order, [q_own, q_other], chunks, spots, state, tok, cache, last=True, ahead=2)
    theirs = moved(theirs, sizes, dc=1)
    return put(place, theirs, result)[None]


def solution(mesh):
    nz, nctx, ntp = mesh.devices.shape
    nx = ny = 4
    nc = nctx // (nx * ny)
    fine = Mesh(mesh.devices.reshape(nz, nx, ny, nc, ntp), ("pipe", "x", "y", "core", "tp"))
    split = P("pipe", ("x", "y", "core"), "tp", None)
    return jax.shard_map(
        functools.partial(on_device, sizes=(nz, nx, ny, nc)),
        mesh=fine,
        in_specs=(split,) * 6 + (P("pipe", None),),
        out_specs=split,
        check_vma=False,
    )
```

```python
import functools
import math

import jax
import jax.numpy as jnp
from jax import lax
from jax.experimental import pallas as pl
from jax.experimental.pallas import tpu as pltpu
from jax.sharding import Mesh, PartitionSpec as P


CBLK = 16
HALF = 32
HD = 128
GROUP = 16
FAR = -(2.0**100)
FLAT = ("pipe", "x", "y", "core")


def moved(value, sizes, dz=0, dx=0, dc=0):
    nz, nx, ny, nc = sizes
    pairs = []
    for z in range(nz):
        for x in range(nx):
            for y in range(ny):
                for c in range(nc):
                    source = ((z * nx + x) * ny + y) * nc + c
                    target = ((((z + dz) % nz) * nx + (x + dx) % nx) * ny + y) * nc + (c ^ dc)
                    pairs.append((source, target))
    return lax.ppermute(value, FLAT, pairs)


def iota(shape, axis):
    return lax.broadcasted_iota(jnp.int32, shape, axis)


def pick(rows, width, first, per_head, heads, scale=None):
    out = iota((rows, width), 0)
    src = iota((rows, width), 1)
    head = first + out // per_head
    token = out % per_head
    hit = src == token * heads + head
    if scale is None:
        return jnp.where(hit, 1.0, 0.0).astype(jnp.bfloat16)
    return jnp.where(hit, scale(token // CBLK, head), 0.0).astype(jnp.bfloat16)


def hadamard_signs():
    bits = iota((HD, HD), 0) & iota((HD, HD), 1)
    bits = bits ^ (bits >> 4)
    bits = bits ^ (bits >> 2)
    bits = (bits ^ (bits >> 1)) & 1
    return (1.0 - 2.0 * bits.astype(jnp.float32)).astype(jnp.bfloat16)


def pack_body(core_ref, exps_ref, order_ref, sk_ref, sv_ref, ck_ref, cv_ref, own_ref, other_ref, *, heads):
    core = core_ref[0]
    tok = sk_ref.shape[0] // heads
    cache = ck_ref.shape[0] // heads
    signs = hadamard_signs()
    for which, ref in ((0, own_ref), (1, other_ref)):
        first = 2 * (core if which == 0 else 1 - core)
        span_pick = pick(2 * tok, heads * tok, first, tok, heads)
        for kv, (span, cached) in enumerate(((sk_ref, ck_ref), (sv_ref, cv_ref))):

            def scale(block, head):
                value = jnp.ones(block.shape, jnp.float32)
                for b in range(cache // CBLK):
                    for h in range(heads):
                        power = (jnp.int32(1) << (exps_ref[b, kv, h] + 3)).astype(jnp.float32) * 0.125
                        value = jnp.where((block == b) & (head == h), power, value)
                return value

            cache_pick = pick(2 * cache, heads * cache, first, cache, heads, scale)
            moved_span = jnp.dot(span_pick, span[...], preferred_element_type=jnp.float32).astype(jnp.bfloat16)
            moved_cache = jnp.dot(cache_pick, cached[...], preferred_element_type=jnp.float32).astype(jnp.bfloat16)
            if kv == 1:
                moved_span = jnp.dot(moved_span, signs, preferred_element_type=jnp.float32).astype(jnp.bfloat16)
                moved_cache = jnp.dot(moved_cache, signs, preferred_element_type=jnp.float32).astype(jnp.bfloat16)
            for h in range(2):
                at = (2 * h + kv) * (cache + tok)
                ref[at : at + cache] = moved_cache[h * cache : (h + 1) * cache]
                ref[at + cache : at + cache + tok] = moved_span[h * tok : (h + 1) * tok]
    order = order_ref[...].astype(jnp.float32)
    order = jnp.concatenate([order, jnp.zeros((1, HD - order.shape[1]), jnp.float32)], axis=1)
    own_ref[4 * (cache + tok) :] = jnp.broadcast_to(order, (16, HD)).astype(jnp.bfloat16)


def pack(core, exps, order, span_keys, span_values, cache_keys, cache_values):
    tok, heads, width = span_keys.shape
    cache = cache_keys.shape[0]
    flat = lambda a: a.reshape(-1, width)
    rows = 4 * (cache + tok)
    smem = pl.BlockSpec(memory_space=pltpu.SMEM)
    vmem = pl.BlockSpec(memory_space=pltpu.VMEM)
    return pl.pallas_call(
        functools.partial(pack_body, heads=heads),
        out_shape=(jax.ShapeDtypeStruct((rows + 16, width), jnp.bfloat16), jax.ShapeDtypeStruct((rows, width), jnp.bfloat16)),
        in_specs=[smem, smem, vmem, vmem, vmem, vmem, vmem],
        out_specs=(vmem, vmem),
        name="pack_kv",
    )(core, exps, order, flat(span_keys), flat(span_values), flat(cache_keys), flat(cache_values))


def fill(place_ref, order_ref, chunk_refs, spots, ka, va, head_slot, tok, cache):
    x, y, core = place_ref[0], place_ref[1], place_ref[2]
    nx, ny = place_ref[3], place_ref[4]
    halves = tok // HALF
    lane = iota((HALF, HD), 1)
    within = iota((HALF, HD), 0)
    slot = lane // HALF
    base = jnp.zeros((HALF, HD), jnp.int32)
    for s in range(2 * halves):
        owner = (x * ny + y) * 2 + (core if s < halves else 1 - core)
        base = jnp.where(slot == s, order_ref[0, owner * halves + s % halves], base)
    pos_query = base * HALF + lane % HALF
    rows = cache + tok
    places = []
    for ref, (shift, first_y) in zip(chunk_refs, spots):
        for k in range(ref.shape[0]):
            for cc in range(2):
                owner = ((x + shift) % nx * ny + first_y + k) * 2 + (core if cc == 0 else 1 - core)
                places.append((ref, k, cc, owner))

    @pl.when(head_slot == 0)
    def _():
        for n, (_, _, _, owner) in enumerate(places):
            at = n * rows
            ka[at : at + cache, HD:] = jnp.zeros((cache, HD), jnp.bfloat16)
            for b in range(halves):
                pos_key = order_ref[0, owner * halves + b] * HALF + within
                start = at + cache + b * HALF
                ka[start : start + HALF, HD:] = jnp.where(pos_key <= pos_query, 0.0, FAR).astype(jnp.bfloat16)
        va[:, HD:] = jnp.ones((va.shape[0], HD), jnp.bfloat16)

    for n, (ref, k, cc, _) in enumerate(places):
        at = n * rows
        ka[at : at + rows, :HD] = ref[k, cc, head_slot, 0]
        va[at : at + rows, :HD] = ref[k, cc, head_slot, 1]


def stage_body(*refs, nchunk, spots, first, last, tok, cache, sub, ahead):
    place_ref, order_ref = refs[0], refs[1]
    refs = refs[2:]
    q_refs, refs = refs[:2], refs[2:]
    chunk_refs, refs = refs[:nchunk], refs[nchunk:]
    if not first:
        (acc_in, max_in), refs = refs[:2], refs[2:]
    if last:
        (own_ref, other_ref), refs = refs[:2], refs[2:]
    else:
        (acc_out, max_out), refs = refs[:2], refs[2:]
    ka, va = refs
    fill(place_ref, order_ref, chunk_refs, spots, ka, va, pl.program_id(0), tok, cache)
    factor = math.log2(math.e) / math.sqrt(HD)
    toks = sub // GROUP
    pieces = 2 * tok // toks

    def scores(s):
        tok0 = s * toks
        ref = q_refs[tok0 // tok]
        part = ref[tok0 % tok : tok0 % tok + toks].reshape(sub, HD)
        token = tok0 + iota((sub, HD), 0) // GROUP
        hot = jnp.where(iota((sub, HD), 1) == token, 1.0, 0.0).astype(jnp.bfloat16)
        left = jnp.concatenate([part, hot], axis=1)
        return lax.dot_general(left, ka[...], (((1,), (1,)), ((), ())), preferred_element_type=jnp.float32)

    ready = [scores(s) for s in range(ahead)]
    for s in range(pieces):
        if s + ahead < pieces:
            ready.append(scores(s + ahead))
        score = ready[s]
        ready[s] = None
        span = slice(s * sub, (s + 1) * sub)
        top = jnp.max(score, axis=1, keepdims=True)
        if not first:
            top_old = max_in[0, span, :1]
            top = jnp.maximum(top, top_old)
        weight = jnp.exp2((score - top) * factor).astype(jnp.bfloat16)
        acc = jnp.dot(weight, va[...], preferred_element_type=jnp.float32)
        if not first:
            acc = acc + acc_in[0, span] * jnp.exp2((top_old - top) * factor)
        if last:
            mixed = acc[:, :HD] * (1.0 / (acc[:, HD:] * math.sqrt(HD)))
            ref = (own_ref, other_ref)[s * toks // tok]
            ref[s * toks % tok : s * toks % tok + toks] = mixed.astype(jnp.bfloat16).reshape(toks, GROUP, HD)
        else:
            acc_out[0, span] = acc
            max_out[0, span] = jnp.broadcast_to(top, (sub, HD))


def stage(place, order, queries, chunks, spots, state, tok, cache, last=False, sub=512, ahead=1):
    total = 2 * tok * GROUP
    keys = sum(c.shape[0] for c in chunks) * 2 * (cache + tok)
    first = state is None
    in_specs = [pl.BlockSpec(memory_space=pltpu.SMEM)]
    for _ in queries:
        in_specs.append(pl.BlockSpec((tok, GROUP, HD), lambda h, p: (0, 2 * p[2] + h, 0)))
    for c in chunks:
        in_specs.append(pl.BlockSpec(c.shape, lambda h, p, nd=c.ndim: (0,) * nd, pipeline_mode=pl.Buffered(1)))
    acc_spec = pl.BlockSpec((1, total, 2 * HD), lambda h, p: (h, 0, 0))
    max_spec = pl.BlockSpec((1, total, HD), lambda h, p: (h, 0, 0))
    operands = [order, *queries, *chunks]
    if not first:
        in_specs += [acc_spec, max_spec]
        operands += list(state)
    if last:
        out_specs = (
            pl.BlockSpec((tok, GROUP, HD), lambda h, p: (0, 2 * p[2] + h, 0)),
            pl.BlockSpec((tok, GROUP, HD), lambda h, p: (0, h, 0)),
        )
        out_shape = (
            jax.ShapeDtypeStruct((tok, 4 * GROUP, HD), jnp.bfloat16),
            jax.ShapeDtypeStruct((tok, 2 * GROUP, HD), jnp.bfloat16),
        )
    else:
        out_specs = (acc_spec, max_spec)
        out_shape = (
            jax.ShapeDtypeStruct((2, total, 2 * HD), jnp.float32),
            jax.ShapeDtypeStruct((2, total, HD), jnp.float32),
        )
    body = functools.partial(
        stage_body, nchunk=len(chunks), spots=spots, first=first, last=last, tok=tok, cache=cache, sub=sub, ahead=ahead
    )
    return pl.pallas_call(
        body,
        grid_spec=pltpu.PrefetchScalarGridSpec(
            num_scalar_prefetch=1,
            grid=(2,),
            in_specs=in_specs,
            out_specs=out_specs,
            scratch_shapes=[pltpu.VMEM((keys, 2 * HD), jnp.bfloat16), pltpu.VMEM((keys, 2 * HD), jnp.bfloat16)],
        ),
        out_shape=out_shape,
        compiler_params=pltpu.CompilerParams(vmem_limit_bytes=24 << 20),
        cost_estimate=pl.CostEstimate(flops=2 * 2 * total * keys * 4 * HD, transcendentals=2 * total * keys, bytes_accessed=12 << 20),
        name="stage_last" if last else "stage",
    )(place, *operands)


def put_body(place_ref, part_ref, whole_ref, out_ref, sems):
    tok, heads = part_ref.shape[:2]
    count = sems.shape[0]
    step = tok // count
    copies = []
    for n in range(count):
        span = pl.ds(n * step, step)
        target = out_ref.at[span, pl.ds((1 - place_ref[2]) * heads, heads)]
        copies.append(pltpu.make_async_copy(part_ref.at[span], target, sems.at[n]))
    for copy in copies:
        copy.start()
    for copy in copies:
        copy.wait()


def put(place, part, whole):
    raw = pl.BlockSpec(memory_space=pl.ANY)
    return pl.pallas_call(
        put_body,
        out_shape=jax.ShapeDtypeStruct(whole.shape, whole.dtype),
        in_specs=[pl.BlockSpec(memory_space=pltpu.SMEM), raw, raw],
        out_specs=raw,
        scratch_shapes=[pltpu.SemaphoreType.DMA((4,))],
        input_output_aliases={2: 0},
        compiler_params=pltpu.CompilerParams(vmem_limit_bytes=1 << 20),
        name="put",
    )(place, part, whole)


def on_device(queries, span_keys, span_values, cache_keys, cache_values, scale_exps, block_order, sizes):
    return relay(queries, span_keys, span_values, cache_keys, cache_values, scale_exps, block_order, sizes)


def relay(queries, span_keys, span_values, cache_keys, cache_values, scale_exps, block_order, sizes):
    _, nx, ny, nc = sizes
    tok, _, width = queries.shape[1:]
    cache = cache_keys.shape[1]
    core = lax.axis_index("core").astype(jnp.int32)
    place = jnp.stack([lax.axis_index("x").astype(jnp.int32), lax.axis_index("y").astype(jnp.int32), core, jnp.int32(nx), jnp.int32(ny)])
    exps = scale_exps[0].transpose(0, 2, 1)
    own, other = pack(core.reshape(1), exps, block_order, span_keys[0], span_values[0], cache_keys[0], cache_values[0])
    own = moved(own, sizes, dz=1)
    other = moved(other, sizes, dz=1, dc=1)
    rows = 4 * (cache + tok)
    order = own[rows : rows + 1, : block_order.shape[1]].astype(jnp.int32)
    q_own = moved(queries[0], sizes, dz=1)
    q_other = moved(q_own, sizes, dc=1)
    mine = jnp.concatenate([own[:rows], other], axis=0)
    line = lax.all_gather(mine, "y", axis=0, tiled=True)
    parts = lambda a: a.reshape(-1, nc, 2, 2, cache + tok, width)
    half = line.shape[0] // 2
    low, high = line[:half], line[half:]
    near_a = moved(low, sizes, dx=1)
    near_b = moved(high, sizes, dx=-1)
    rest_a = moved(high, sizes, dx=1)
    rest_b = moved(low, sizes, dx=-1)
    far_a = moved(near_a, sizes, dx=1)
    far_b = moved(near_b, sizes, dx=-1)
    mid = ny // 2
    spots = [(0, 0), (nx - 1, 0), (1, mid)]
    state = stage(place, order, [q_own, q_other], [parts(line), parts(near_a), parts(near_b)], spots, None, tok, cache)
    chunks = [parts(rest_a), parts(rest_b), parts(far_a), parts(far_b)]
    spots = [(nx - 1, mid), (1, 0), (2, 0), (2, mid)]
    result, theirs = stage(place, order, [q_own, q_other], chunks, spots, state, tok, cache, last=True, ahead=3)
    theirs = moved(theirs, sizes, dc=1)
    return put(place, theirs, result)[None]


def solution(mesh):
    nz, nctx, ntp = mesh.devices.shape
    nx = ny = 4
    nc = nctx // (nx * ny)
    fine = Mesh(mesh.devices.reshape(nz, nx, ny, nc, ntp), ("pipe", "x", "y", "core", "tp"))
    split = P("pipe", ("x", "y", "core"), "tp", None)
    return jax.shard_map(
        functools.partial(on_device, sizes=(nz, nx, ny, nc)),
        mesh=fine,
        in_specs=(split,) * 6 + (P("pipe", None),),
        out_specs=split,
        check_vma=False,
    )
```

```python
import functools
import math

import jax
import jax.numpy as jnp
from jax import lax
from jax.experimental import pallas as pl
from jax.experimental.pallas import tpu as pltpu
from jax.sharding import Mesh, PartitionSpec as P


CBLK = 16
HALF = 32
HD = 128
GROUP = 16
FAR = -(2.0**100)
FLAT = ("pipe", "x", "y", "core")


def moved(value, sizes, dz=0, dx=0, dc=0):
    nz, nx, ny, nc = sizes
    pairs = []
    for z in range(nz):
        for x in range(nx):
            for y in range(ny):
                for c in range(nc):
                    source = ((z * nx + x) * ny + y) * nc + c
                    target = ((((z + dz) % nz) * nx + (x + dx) % nx) * ny + y) * nc + (c ^ dc)
                    pairs.append((source, target))
    return lax.ppermute(value, FLAT, pairs)


def iota(shape, axis):
    return lax.broadcasted_iota(jnp.int32, shape, axis)


def pick(rows, width, first, per_head, heads, scale=None):
    out = iota((rows, width), 0)
    src = iota((rows, width), 1)
    head = first + out // per_head
    token = out % per_head
    hit = src == token * heads + head
    if scale is None:
        return jnp.where(hit, 1.0, 0.0).astype(jnp.bfloat16)
    return jnp.where(hit, scale(token // CBLK, head), 0.0).astype(jnp.bfloat16)


def hadamard_signs():
    bits = iota((HD, HD), 0) & iota((HD, HD), 1)
    bits = bits ^ (bits >> 4)
    bits = bits ^ (bits >> 2)
    bits = (bits ^ (bits >> 1)) & 1
    return (1.0 - 2.0 * bits.astype(jnp.float32)).astype(jnp.bfloat16)


def pack_body(core_ref, exps_ref, order_ref, sk_ref, sv_ref, ck_ref, cv_ref, own_ref, other_ref, *, heads):
    core = core_ref[0]
    tok = sk_ref.shape[0] // heads
    cache = ck_ref.shape[0] // heads
    signs = hadamard_signs()
    for which, ref in ((0, own_ref), (1, other_ref)):
        first = 2 * (core if which == 0 else 1 - core)
        span_pick = pick(2 * tok, heads * tok, first, tok, heads)
        for kv, (span, cached) in enumerate(((sk_ref, ck_ref), (sv_ref, cv_ref))):

            def scale(block, head):
                value = jnp.ones(block.shape, jnp.float32)
                for b in range(cache // CBLK):
                    for h in range(heads):
                        power = (jnp.int32(1) << (exps_ref[b, kv, h] + 3)).astype(jnp.float32) * 0.125
                        value = jnp.where((block == b) & (head == h), power, value)
                return value

            cache_pick = pick(2 * cache, heads * cache, first, cache, heads, scale)
            moved_span = jnp.dot(span_pick, span[...], preferred_element_type=jnp.float32).astype(jnp.bfloat16)
            moved_cache = jnp.dot(cache_pick, cached[...], preferred_element_type=jnp.float32).astype(jnp.bfloat16)
            if kv == 1:
                moved_span = jnp.dot(moved_span, signs, preferred_element_type=jnp.float32).astype(jnp.bfloat16)
                moved_cache = jnp.dot(moved_cache, signs, preferred_element_type=jnp.float32).astype(jnp.bfloat16)
            for h in range(2):
                at = (2 * h + kv) * (cache + tok)
                ref[at : at + cache] = moved_cache[h * cache : (h + 1) * cache]
                ref[at + cache : at + cache + tok] = moved_span[h * tok : (h + 1) * tok]
    order = order_ref[...].astype(jnp.float32)
    order = jnp.concatenate([order, jnp.zeros((1, HD - order.shape[1]), jnp.float32)], axis=1)
    own_ref[4 * (cache + tok) :] = jnp.broadcast_to(order, (16, HD)).astype(jnp.bfloat16)


def pack(core, exps, order, span_keys, span_values, cache_keys, cache_values):
    tok, heads, width = span_keys.shape
    cache = cache_keys.shape[0]
    flat = lambda a: a.reshape(-1, width)
    rows = 4 * (cache + tok)
    smem = pl.BlockSpec(memory_space=pltpu.SMEM)
    vmem = pl.BlockSpec(memory_space=pltpu.VMEM)
    return pl.pallas_call(
        functools.partial(pack_body, heads=heads),
        out_shape=(jax.ShapeDtypeStruct((rows + 16, width), jnp.bfloat16), jax.ShapeDtypeStruct((rows, width), jnp.bfloat16)),
        in_specs=[smem, smem, vmem, vmem, vmem, vmem, vmem],
        out_specs=(vmem, vmem),
        name="pack_kv",
    )(core, exps, order, flat(span_keys), flat(span_values), flat(cache_keys), flat(cache_values))


def fill(place_ref, order_ref, chunk_refs, spots, ka, va, head_slot, tok, cache):
    x, y, core = place_ref[0], place_ref[1], place_ref[2]
    nx, ny = place_ref[3], place_ref[4]
    halves = tok // HALF
    lane = iota((HALF, HD), 1)
    within = iota((HALF, HD), 0)
    slot = lane // HALF
    base = jnp.zeros((HALF, HD), jnp.int32)
    for s in range(2 * halves):
        owner = (x * ny + y) * 2 + (core if s < halves else 1 - core)
        base = jnp.where(slot == s, order_ref[0, owner * halves + s % halves], base)
    pos_query = base * HALF + lane % HALF
    rows = cache + tok
    places = []
    for ref, (shift, first_y) in zip(chunk_refs, spots):
        for k in range(ref.shape[0]):
            for cc in range(2):
                owner = ((x + shift) % nx * ny + first_y + k) * 2 + (core if cc == 0 else 1 - core)
                places.append((ref, k, cc, owner))

    @pl.when(head_slot == 0)
    def _():
        for n, (_, _, _, owner) in enumerate(places):
            at = n * rows
            ka[at : at + cache, HD:] = jnp.zeros((cache, HD), jnp.bfloat16)
            for b in range(halves):
                pos_key = order_ref[0, owner * halves + b] * HALF + within
                start = at + cache + b * HALF
                ka[start : start + HALF, HD:] = jnp.where(pos_key <= pos_query, 0.0, FAR).astype(jnp.bfloat16)
        va[:, HD:] = jnp.ones((va.shape[0], HD), jnp.bfloat16)

    for n, (ref, k, cc, _) in enumerate(places):
        at = n * rows
        ka[at : at + rows, :HD] = ref[k, cc, head_slot, 0]
        va[at : at + rows, :HD] = ref[k, cc, head_slot, 1]


def stage_body(*refs, nchunk, spots, first, last, tok, cache, sub, ahead):
    place_ref, order_ref = refs[0], refs[1]
    refs = refs[2:]
    q_refs, refs = refs[:2], refs[2:]
    chunk_refs, refs = refs[:nchunk], refs[nchunk:]
    if not first:
        (acc_in, max_in), refs = refs[:2], refs[2:]
    if last:
        (own_ref, other_ref), refs = refs[:2], refs[2:]
    else:
        (acc_out, max_out), refs = refs[:2], refs[2:]
    ka, va = refs
    fill(place_ref, order_ref, chunk_refs, spots, ka, va, pl.program_id(0), tok, cache)
    factor = math.log2(math.e) / math.sqrt(HD)
    toks = sub // GROUP
    pieces = 2 * tok // toks

    def scores(s):
        tok0 = s * toks
        ref = q_refs[tok0 // tok]
        part = ref[tok0 % tok : tok0 % tok + toks].reshape(sub, HD)
        token = tok0 + iota((sub, HD), 0) // GROUP
        hot = jnp.where(iota((sub, HD), 1) == token, 1.0, 0.0).astype(jnp.bfloat16)
        left = jnp.concatenate([part, hot], axis=1)
        return lax.dot_general(left, ka[...], (((1,), (1,)), ((), ())), preferred_element_type=jnp.float32)

    ready = [scores(s) for s in range(ahead)]
    for s in range(pieces):
        if s + ahead < pieces:
            ready.append(scores(s + ahead))
        score = ready[s]
        ready[s] = None
        span = slice(s * sub, (s + 1) * sub)
        top = jnp.max(score, axis=1, keepdims=True)
        if not first:
            top_old = max_in[0, span, :1]
            top = jnp.maximum(top, top_old)
        weight = jnp.exp2((score - top) * factor).astype(jnp.bfloat16)
        acc = jnp.dot(weight, va[...], preferred_element_type=jnp.float32)
        if not first:
            acc = acc + acc_in[0, span] * jnp.exp2((top_old - top) * factor)
        if last:
            mixed = acc[:, :HD] * (1.0 / (acc[:, HD:] * math.sqrt(HD)))
            ref = (own_ref, other_ref)[s * toks // tok]
            ref[s * toks % tok : s * toks % tok + toks] = mixed.astype(jnp.bfloat16).reshape(toks, GROUP, HD)
        else:
            acc_out[0, span] = acc
            max_out[0, span] = jnp.broadcast_to(top, (sub, HD))


def stage(place, order, queries, chunks, spots, state, tok, cache, last=False, sub=512, ahead=1):
    total = 2 * tok * GROUP
    keys = sum(c.shape[0] for c in chunks) * 2 * (cache + tok)
    first = state is None
    in_specs = [pl.BlockSpec(memory_space=pltpu.SMEM)]
    for _ in queries:
        in_specs.append(pl.BlockSpec((tok, GROUP, HD), lambda h, p: (0, 2 * p[2] + h, 0)))
    for c in chunks:
        in_specs.append(pl.BlockSpec(c.shape, lambda h, p, nd=c.ndim: (0,) * nd, pipeline_mode=pl.Buffered(1)))
    acc_spec = pl.BlockSpec((1, total, 2 * HD), lambda h, p: (h, 0, 0))
    max_spec = pl.BlockSpec((1, total, HD), lambda h, p: (h, 0, 0))
    operands = [order, *queries, *chunks]
    if not first:
        in_specs += [acc_spec, max_spec]
        operands += list(state)
    if last:
        out_specs = (
            pl.BlockSpec((tok, GROUP, HD), lambda h, p: (0, 2 * p[2] + h, 0)),
            pl.BlockSpec((tok, GROUP, HD), lambda h, p: (0, h, 0)),
        )
        out_shape = (
            jax.ShapeDtypeStruct((tok, 4 * GROUP, HD), jnp.bfloat16),
            jax.ShapeDtypeStruct((tok, 2 * GROUP, HD), jnp.bfloat16),
        )
    else:
        out_specs = (acc_spec, max_spec)
        out_shape = (
            jax.ShapeDtypeStruct((2, total, 2 * HD), jnp.float32),
            jax.ShapeDtypeStruct((2, total, HD), jnp.float32),
        )
    body = functools.partial(
        stage_body, nchunk=len(chunks), spots=spots, first=first, last=last, tok=tok, cache=cache, sub=sub, ahead=ahead
    )
    return pl.pallas_call(
        body,
        grid_spec=pltpu.PrefetchScalarGridSpec(
            num_scalar_prefetch=1,
            grid=(2,),
            in_specs=in_specs,
            out_specs=out_specs,
            scratch_shapes=[pltpu.VMEM((keys, 2 * HD), jnp.bfloat16), pltpu.VMEM((keys, 2 * HD), jnp.bfloat16)],
        ),
        out_shape=out_shape,
        compiler_params=pltpu.CompilerParams(vmem_limit_bytes=24 << 20),
        cost_estimate=pl.CostEstimate(flops=2 * 2 * total * keys * 4 * HD, transcendentals=2 * total * keys, bytes_accessed=12 << 20),
        name="stage_last" if last else "stage",
    )(place, *operands)


def on_device(queries, span_keys, span_values, cache_keys, cache_values, scale_exps, block_order, sizes):
    return relay(queries, span_keys, span_values, cache_keys, cache_values, scale_exps, block_order, sizes)


def relay(queries, span_keys, span_values, cache_keys, cache_values, scale_exps, block_order, sizes):
    _, nx, ny, nc = sizes
    tok, _, width = queries.shape[1:]
    cache = cache_keys.shape[1]
    core = lax.axis_index("core").astype(jnp.int32)
    place = jnp.stack([lax.axis_index("x").astype(jnp.int32), lax.axis_index("y").astype(jnp.int32), core, jnp.int32(nx), jnp.int32(ny)])
    exps = scale_exps[0].transpose(0, 2, 1)
    own, other = pack(core.reshape(1), exps, block_order, span_keys[0], span_values[0], cache_keys[0], cache_values[0])
    own = moved(own, sizes, dz=1)
    other = moved(other, sizes, dz=1, dc=1)
    rows = 4 * (cache + tok)
    order = own[rows : rows + 1, : block_order.shape[1]].astype(jnp.int32)
    q_own = moved(queries[0], sizes, dz=1)
    q_other = moved(q_own, sizes, dc=1)
    mine = jnp.concatenate([own[:rows], other], axis=0)
    line = lax.all_gather(mine, "y", axis=0, tiled=True)
    parts = lambda a: a.reshape(-1, nc, 2, 2, cache + tok, width)
    half = line.shape[0] // 2
    low, high = line[:half], line[half:]
    near_a = moved(low, sizes, dx=1)
    near_b = moved(high, sizes, dx=-1)
    rest_a = moved(high, sizes, dx=1)
    rest_b = moved(low, sizes, dx=-1)
    far_a = moved(near_a, sizes, dx=1)
    far_b = moved(near_b, sizes, dx=-1)
    mid = ny // 2
    spots = [(0, 0), (nx - 1, 0), (1, mid)]
    state = stage(place, order, [q_own, q_other], [parts(line), parts(near_a), parts(near_b)], spots, None, tok, cache)
    chunks = [parts(rest_a), parts(rest_b), parts(far_a), parts(far_b)]
    spots = [(nx - 1, mid), (1, 0), (2, 0), (2, mid)]
    result, theirs = stage(place, order, [q_own, q_other], chunks, spots, state, tok, cache, last=True, ahead=3)
    theirs = moved(theirs, sizes, dc=1)
    return lax.dynamic_update_slice(result, theirs, (0, (1 - core) * theirs.shape[1], 0))[None]


def solution(mesh):
    nz, nctx, ntp = mesh.devices.shape
    nx = ny = 4
    nc = nctx // (nx * ny)
    fine = Mesh(mesh.devices.reshape(nz, nx, ny, nc, ntp), ("pipe", "x", "y", "core", "tp"))
    split = P("pipe", ("x", "y", "core"), "tp", None)
    return jax.shard_map(
        functools.partial(on_device, sizes=(nz, nx, ny, nc)),
        mesh=fine,
        in_specs=(split,) * 6 + (P("pipe", None),),
        out_specs=split,
        check_vma=False,
    )
```
